32 devices in a mesh: segment: 2 (over core), grp: 16 (over z, y, x).
Axes of the slice: x: 2, y: 2, z: 4, core: 2. Of those that a mesh axis runs over, the one named last changes fastest.
Arguments:
- monomer_density: bfloat16 [128, 9216], P('grp'), may hold values from -3 to 3
- monomer_centers: float32 [3, 128], replicated, may hold values from 0 to 8
- dimer_pairs: int32 [2, 256], replicated, may hold values from 0 to 127, as said below
- basis_sizes: int32 [128], replicated, may hold values from 48 to 96
- dimer_core: float32 [256, 36864], P('grp')
- esp_map: float32 [96, 192], replicated, may hold values from -0.1875 to 0.1875
- repulsion: float32 [36864], replicated, may hold values from 0.005 to 0.05
Outputs:
- section_out: float32 [2, 256, 36864], P('segment', 'grp')
- window_energy: float32 [], replicated
The draws below stay inside these ranges and needn't reach their ends.
Inputs may be any that keep to these rules, and one draw needn't show every extreme that they name: `dimer_pairs`: the two monomers of a dimer differ.
All inputs are finite; a program needn't handle non-finite values. Where the reference program divides by a largest or mean magnitude, that divisor is 1e-20 or more.
Results may differ from the reference program's by a relative error of at most 0.00045.
Values may be sent and summed in bfloat16 or wider, within the bound.
A program may use at most 128 MiB of HBM per device.

```python
import jax
import jax.numpy as jnp
from jax import lax

BM = 96
BD = 192
SCF_ITERS = 1
PURIFY = 8
DIMS_DEV = 16
NMON = 128
NDIM = 256


def draw_dimer_pairs(key, part):
    first_key, second_key = jax.random.split(jax.random.fold_in(key, 11))
    first_ids = jax.random.randint(first_key, (NDIM,), 0, NMON)
    offsets = jax.random.randint(second_key, (NDIM,), 1, NMON)
    second_ids = (first_ids + offsets) % NMON
    return jnp.stack([first_ids, second_ids]).astype(jnp.int32)


def draw_dimer_core(key, part):
    base_key, onsite_key = jax.random.split(jax.random.fold_in(key, 23), 2)
    coupling = 0.15 * jax.random.normal(base_key, (NDIM, BD, BD), jnp.float32)
    onsite = jax.random.uniform(onsite_key, (NDIM, BD), jnp.float32, -1.5, 1.5)
    identity = jnp.eye(BD, dtype=jnp.float32)
    square = coupling + onsite[:, :, None] * identity
    return square.reshape(NDIM, BD * BD).astype(jnp.float32)


def plant(entries, own_key, smallest, largest):
    extent = entries.shape
    place = [jax.random.randint(jax.random.fold_in(own_key, axis), (), 0, extent[axis]) for axis in range(len(extent))]
    entries = entries.at[tuple(place)].set(smallest)
    longest = extent.index(max(extent))
    place[longest] = (place[longest] + 1) % extent[longest]
    return entries.at[tuple(place)].set(largest)


def shard_levels(own_key, dims, shards, least, high):
    level = 1.0
    for dim, parts in shards:
        steps = jax.random.uniform(jax.random.fold_in(jax.random.fold_in(own_key, 6), dim), (parts,), jnp.float32, least / len(shards), high / len(shards))
        level = level * jnp.repeat(jnp.exp(steps), dims[dim] // parts).reshape((-1,) + (1,) * (len(dims) - 1 - dim))
    return level


def scatter_about(own_key, dims, deviation, bound, shards=(), kind=jnp.bfloat16):
    factor_of = shard_levels(own_key, dims, shards, -0.22, 0.18) if shards else 1.0
    result = jax.random.normal(own_key, dims, jnp.float32) * deviation * factor_of
    return jnp.minimum(jnp.maximum(result, -bound), bound).astype(kind)


def setup_inputs(seed: int = 0) -> dict:
    splits = jax.random.split(jax.random.key(seed), 8)
    return {
        "monomer_density": scatter_about(splits[0], (NMON, BM * BM), 0.5, 3.0, ((0, 16),)),
        "monomer_centers": jnp.clip(jax.random.uniform(splits[1], (3, NMON), jnp.float32, 0.0, 8.0), 0.0, 8.0),
        "dimer_pairs": draw_dimer_pairs(jax.random.fold_in(splits[7], 71), 0),
        "basis_sizes": plant(jax.random.randint(splits[3], (NMON,), BM // 2, BM + 1), jax.random.fold_in(splits[3], 1), BM // 2, BM).astype(jnp.int32),
        "dimer_core": draw_dimer_core(jax.random.fold_in(splits[7], 71), 0),
        "esp_map": scatter_about(splits[5], (BM, BD), (BM * 12) ** -0.5, 0.1875, (), jnp.float32),
        "repulsion": jnp.clip(jax.random.uniform(splits[6], (BD * BD,), jnp.float32, 0.005, 0.05), 0.005, 0.05),
    }


epsilon = 1e-06
highest = lax.Precision.HIGHEST

def esp_weights(first_ids, second_ids, centers, first_row, row_count):
    nearby = lax.dynamic_slice_in_dim(centers, first_row, row_count, 1)
    middle = 0.5 * (centers[:, first_ids] + centers[:, second_ids])
    distance = jnp.zeros((first_ids.shape[0], row_count), jnp.float32)
    for axis_pos in range(3):
        axis_gap = middle[axis_pos][:, None] - nearby[axis_pos][None, :]
        distance = distance + axis_gap * axis_gap
    weights = 1.0 / jnp.sqrt(distance + 1.0)
    labels = first_row + jnp.arange(row_count, dtype=jnp.int32)
    excluded = (labels[None, :] == first_ids[:, None]) | (labels[None, :] == second_ids[:, None])
    return jnp.where(excluded, 0.0, weights)

def live_masks(first_ids, second_ids, basis_sizes, width):
    first_size = basis_sizes[first_ids]
    second_size = basis_sizes[second_ids]
    position = jnp.arange(2 * width, dtype=jnp.int32)
    inside = jnp.where(position[None, :] < width, position[None, :] < first_size[:, None], position[None, :] - width < second_size[:, None])
    return inside.astype(jnp.float32)

def embedded(field_sum, core_rows, esp_map):
    row_count = core_rows.shape[0]
    width = esp_map.shape[0]
    field = field_sum.reshape(row_count, width, width)
    field = 0.5 * (field + jnp.swapaxes(field, 1, 2))
    left_side = jnp.einsum('am,kab->kmb', esp_map, field, precision=highest)
    potential = jnp.einsum('kmb,bn->kmn', left_side, esp_map, precision=highest)
    return 0.5 * (core_rows + jnp.swapaxes(core_rows, 1, 2)) + potential

def purify(fock_matrix, live_mask):
    pair_mask = live_mask[:, :, None] * live_mask[:, None, :]
    masked = fock_matrix * pair_mask
    identity = jnp.eye(fock_matrix.shape[1], dtype=jnp.float32)
    live_diag = live_mask[:, :, None] * identity
    chemical = lax.optimization_barrier(jnp.sum(masked * identity, axis=(1, 2))) / lax.optimization_barrier(jnp.sum(live_mask, axis=1))
    shifted = masked - chemical[:, None, None] * live_diag
    radius = lax.optimization_barrier(jnp.max(lax.optimization_barrier(jnp.sum(jnp.abs(shifted), axis=2)), axis=1))
    scaling = 0.5 / (radius + epsilon)
    density = 0.5 * live_diag - scaling[:, None, None] * shifted
    for repeat in range(PURIFY):
        squared = jnp.einsum('kab,kbc->kac', density, density, precision=highest)
        density = 3.0 * squared - 2.0 * jnp.einsum('kab,kbc->kac', squared, density, precision=highest)
    return density

def fock_update(core_fock, density, repulsion):
    symmetric = 0.5 * (repulsion + repulsion.T)
    occupied = jnp.diagonal(density, axis1=1, axis2=2)
    coulomb = jnp.dot(occupied, symmetric, precision=highest)
    identity = jnp.eye(density.shape[1], dtype=jnp.float32)
    return core_fock + coulomb[:, :, None] * identity - 0.5 * symmetric[None] * density

def scf_solve(core_fock, live_mask, repulsion):
    density = purify(core_fock, live_mask)
    fock_matrix = core_fock
    for repeat in range(SCF_ITERS):
        fock_matrix = fock_update(core_fock, density, repulsion)
        density = purify(fock_matrix, live_mask)
    energy = 0.5 * lax.optimization_barrier(jnp.sum(density * (core_fock + fock_matrix), axis=(1, 2))) / lax.optimization_barrier(jnp.sum(live_mask, axis=1))
    return (density, energy)

def reference(monomer_density, monomer_centers, dimer_pairs, basis_sizes, dimer_core, esp_map, repulsion):
    monomers = monomer_density.shape[0]
    width = esp_map.shape[0]
    full = esp_map.shape[1]
    first_ids = dimer_pairs[0].astype(jnp.int32)
    second_ids = dimer_pairs[1].astype(jnp.int32)
    weights = esp_weights(first_ids, second_ids, monomer_centers, jnp.int32(0), monomers).astype(jnp.bfloat16)
    field_sum = jnp.dot(weights, monomer_density, preferred_element_type=jnp.float32)
    core_square = dimer_core.reshape(dimer_core.shape[0], full, full)
    repulsion_square = repulsion.reshape(full, full)
    core_fock = embedded(field_sum, core_square, esp_map)
    live_mask = live_masks(first_ids, second_ids, basis_sizes, width)
    groups = core_fock.shape[0] // DIMS_DEV

    def solve_group(operands):
        return scf_solve(operands[0], operands[1], repulsion_square)
    density, energy = lax.map(solve_group, (core_fock.reshape(groups, DIMS_DEV, full, full), live_mask.reshape(groups, DIMS_DEV, full)))
    section_out = jnp.stack([core_fock.reshape(-1, full * full), density.reshape(-1, full * full)])
    window_energy = jnp.sum(energy) / core_fock.shape[0]
    return (section_out, window_energy)
```

```python
import functools

import jax
import jax.numpy as jnp
from jax import lax
from jax.experimental import pallas as pl
from jax.experimental.pallas import tpu as pltpu
from jax.sharding import PartitionSpec as P

PURIFY = 8
epsilon = 1e-06
LANES = 128
MESH = pl.DeviceIdType.MESH
FIRST_PLAN = ((1, 1),) * PURIFY
LAST_PLAN = ((1, 1),) * (PURIFY - 3) + ((3, 3),) * 3


def flow_orders(groups):
    top, *rest = reversed([1 << k for k in range(groups.bit_length() - 1)])
    return [[top] + rest[f * len(rest) // 3:] + rest[:f * len(rest) // 3] for f in range(3)]


def bf(value):
    return value.astype(jnp.bfloat16)


def dot(left, right):
    return jnp.dot(left, right, preferred_element_type=jnp.float32)


def split(value):
    high = bf(value)
    return high, bf(value - high.astype(jnp.float32))


def product(left, right, passes):
    if passes == 1:
        return dot(bf(left), bf(right))
    left_high, left_low = split(left)
    right_high, right_low = split(right)
    return dot(left_high, right_high) + (dot(left_high, right_low) + dot(left_low, right_high))


def iota(shape, axis):
    return lax.broadcasted_iota(jnp.int32, shape, axis)


def pair_ids(pairs_ref, positions):
    count = positions.shape[0]
    hit = iota((count, pairs_ref.shape[1]), 1) == positions
    out = []
    for side in range(2):
        row = pairs_ref[side:side + 1, :].astype(jnp.float32)
        out.append(jnp.sum(jnp.where(hit, row, 0.0), axis=1, keepdims=True).astype(jnp.int32))
    return out


def field_kernel(groups, density_ref, centers_ref, pairs_ref, field_ref, blocks, staged, send_sem, recv_sem, own_sem, part_send, part_recv, out_sem):
    me = lax.axis_index("grp")
    seg = lax.axis_index("segment")
    rows, total = density_ref.shape
    orders = flow_orders(groups)
    flows = len(orders)
    stages = len(orders[0])
    half = total // 2
    width = half // flows
    tiles = half // LANES
    monomers = centers_ref.shape[1]
    dims = pairs_ref.shape[1] // groups
    mine = dims // 2

    barrier = pltpu.get_barrier_semaphore()
    for bit in sorted(orders[0]):
        pl.semaphore_signal(barrier, inc=1, device_id=(seg, me ^ bit), device_id_type=MESH)
    pl.semaphore_signal(barrier, inc=1, device_id=(1 - seg, me), device_id_type=MESH)

    own = []
    for f in range(flows):
        start = pl.multiple_of(seg * half + f * width, LANES)
        source = density_ref.at[:, pl.ds(start, width)]
        copy = pltpu.make_async_copy(source, blocks.at[f, 0], own_sem.at[f])
        copy.start()
        own.append(copy)
    pl.semaphore_wait(barrier, stages + 1)

    def exchange(f, k):
        count = 1 << k
        return pltpu.make_async_remote_copy(
            src_ref=blocks.at[f, pl.ds(0, count)],
            dst_ref=blocks.at[f, pl.ds(count, count)],
            send_sem=send_sem.at[f, k],
            recv_sem=recv_sem.at[f, k],
            device_id=(seg, me ^ orders[f][k]),
            device_id_type=MESH,
        )

    for f in range(flows):
        own[f].wait()
        exchange(f, 0).start()

    place = iota((dims, 1), 0)
    is_own = place < mine
    positions = me * dims + jnp.where(is_own, seg * mine + place, (1 - seg) * mine + place - mine)
    first_ids, second_ids = pair_ids(pairs_ref, positions)
    labels = iota((dims, monomers), 1)
    is_first = labels == first_ids
    is_second = labels == second_ids
    distance = jnp.zeros((dims, monomers), jnp.float32)
    for axis in range(centers_ref.shape[0]):
        row = centers_ref[axis:axis + 1, :]
        first_at = jnp.sum(jnp.where(is_first, row, 0.0), axis=1, keepdims=True)
        second_at = jnp.sum(jnp.where(is_second, row, 0.0), axis=1, keepdims=True)
        gap = 0.5 * (first_at + second_at) - row
        distance = distance + gap * gap
    weights = jnp.where(is_first | is_second, 0.0, 1.0 / jnp.sqrt(distance + 1.0))
    weights = bf(weights)
    ordered = []
    for f in range(flows):
        column = iota((monomers, monomers), 1)
        slot = column // rows
        owner = jnp.full_like(column, me)
        for k, bit in enumerate(orders[f]):
            owner = owner ^ jnp.where((slot & (1 << k)) != 0, bit, 0)
        label = owner * rows + (column & (rows - 1))
        chosen = bf(jnp.where(iota((monomers, monomers), 0) == label, 1.0, 0.0))
        ordered.append(bf(dot(weights, chosen)))

    for k in range(1, stages):
        for f in range(flows):
            exchange(f, k - 1).wait()
            exchange(f, k).start()

    for f in range(flows):
        exchange(f, stages - 1).wait()
        gathered = bf(blocks[f].astype(jnp.float32).reshape(monomers, width))
        result = dot(ordered[f], gathered)
        for t in range(width // LANES):
            piece = result[:, t * LANES:(t + 1) * LANES]
            staged[0, f * (width // LANES) + t] = piece[:mine]
            staged[1, f * (width // LANES) + t] = piece[mine:]

    target = field_ref.at[pl.ds(seg * tiles, tiles)]
    give = pltpu.make_async_remote_copy(
        src_ref=staged.at[1], dst_ref=target, send_sem=part_send, recv_sem=part_recv,
        device_id=(1 - seg, me), device_id_type=MESH,
    )
    give.start()
    keep = pltpu.make_async_copy(staged.at[0], target, out_sem)
    keep.start()
    keep.wait()
    give.wait()


def make_field(groups, density, centers, pairs):
    rows, total = density.shape
    flows = len(flow_orders(groups))
    stages = groups.bit_length() - 1
    half = total // 2
    mine = pairs.shape[1] // groups // 2
    vmem = pl.BlockSpec(memory_space=pltpu.VMEM)
    return pl.pallas_call(
        functools.partial(field_kernel, groups),
        out_shape=jax.ShapeDtypeStruct((total // LANES, mine, LANES), jnp.float32),
        in_specs=[pl.BlockSpec(memory_space=pl.ANY), vmem, vmem],
        out_specs=vmem,
        scratch_shapes=[
            pltpu.VMEM((flows, groups, rows, half // flows), jnp.bfloat16),
            pltpu.VMEM((2, half // LANES, mine, LANES), jnp.float32),
            pltpu.SemaphoreType.DMA((flows, stages)),
            pltpu.SemaphoreType.DMA((flows, stages)),
            pltpu.SemaphoreType.DMA((flows,)),
            pltpu.SemaphoreType.DMA,
            pltpu.SemaphoreType.DMA,
            pltpu.SemaphoreType.DMA,
        ],
        compiler_params=pltpu.CompilerParams(collective_id=0, has_side_effects=True),
    )(density, centers, pairs)


def rolled(value, shift):
    return pltpu.roll(value, shift, 1)


def load_field(field_ref, buffer, d, mine, width):
    count = width * width // LANES // 3
    a, b, c = [field_ref[pl.ds(j * mine + d, count, stride=3 * mine), :] for j in range(3)]
    lane = iota((count, LANES), 1)
    buffer[pl.ds(0, count, stride=4), :] = a
    buffer[pl.ds(1, count, stride=4), :] = jnp.where(lane < 32, rolled(a, 32), rolled(b, 32))
    buffer[pl.ds(2, count, stride=4), :] = jnp.where(lane < 64, rolled(b, 64), rolled(c, 64))
    buffer[pl.ds(3, count, stride=4), :] = rolled(c, 96)
    return buffer[:, :width]


def load_square(source, low, high, d, mine, full):
    count = full // 2
    a, b, c = [source[pl.ds(j * mine + d, count, stride=3 * mine), :] for j in range(3)]
    lane = iota((count, LANES), 1)
    shifted = rolled(c, 64)
    low[pl.ds(0, count, stride=2), :] = a
    high[pl.ds(0, count, stride=2), :] = b
    low[pl.ds(1, count, stride=2), :] = jnp.where(lane < 64, rolled(b, 64), shifted)
    high[pl.ds(1, count, stride=2), :] = shifted
    return jnp.concatenate([low[...], high[:, :full - LANES]], axis=1)


def store_square(target, value, low, high, d, mine, full):
    count = full // 2
    low[...] = value[:, :LANES]
    high[:, :full - LANES] = value[:, LANES:]
    lane = iota((count, LANES), 1)
    even_low = low[pl.ds(0, count, stride=2), :]
    even_high = high[pl.ds(0, count, stride=2), :]
    odd_low = rolled(low[pl.ds(1, count, stride=2), :], 64)
    odd_high = rolled(high[pl.ds(1, count, stride=2), :], 64)
    pieces = (even_low, jnp.where(lane < 64, even_high, odd_low), jnp.where(lane < 64, odd_low, odd_high))
    for j, piece in enumerate(pieces):
        target[pl.ds(j * mine + d, count, stride=3 * mine), :] = piece


def solve_kernel(groups, field_ref, sizes_ref, pairs_ref, core_ref, map_ref, rep_ref, section_ref, energy_ref, core_buf, low, high, fbuf, fock, iterate, core_sem):
    me = lax.axis_index("grp")
    seg = lax.axis_index("segment")
    width, full = map_ref.shape
    dims = pairs_ref.shape[1] // groups
    mine = dims // 2
    fetch = pltpu.make_async_copy(core_ref.at[seg], core_buf, core_sem)
    fetch.start()

    positions = me * dims + seg * mine + iota((mine, 1), 0)
    ids = pair_ids(pairs_ref, positions)
    labels = iota((mine, sizes_ref.shape[1]), 1)
    sizes = [
        jnp.sum(jnp.where(labels == i, sizes_ref[...].astype(jnp.float32), 0.0), axis=1, keepdims=True)
        for i in ids
    ]
    row_at = iota((1, full), 1)
    column_at = iota((full, 1), 0)
    eye = iota((full, full), 0) == iota((full, full), 1)
    rep_low, rep_high = low.at[0], high.at[0]
    repulsion = load_square(rep_ref, rep_low, rep_high, 0, 1, full)
    symmetric = 0.5 * (repulsion + repulsion.T)
    mapping = map_ref[...]
    mapping_t = mapping.T

    def live(d):
        first, second = [s[d:d + 1, :] for s in sizes]
        out = []
        for at in (row_at, column_at):
            limit = jnp.where(at < width, first, second + width)
            out.append(jnp.where(at.astype(jnp.float32) < limit, 1.0, 0.0))
        return out, first + second

    def total(value):
        return jnp.sum(jnp.sum(value, axis=0, keepdims=True), axis=1, keepdims=True)

    def begin(matrix, d):
        (live_row, live_column), count = live(d)
        masked = matrix * (live_column * live_row)
        chemical = total(jnp.where(eye, masked, 0.0)) / count
        shifted = masked - jnp.where(eye, chemical * live_row, 0.0)
        radius = jnp.max(jnp.sum(jnp.abs(shifted), axis=0, keepdims=True), axis=1, keepdims=True)
        iterate[d] = shifted * (-1.0 / (radius + epsilon))

    def step(passes):
        first, second = passes
        values = [iterate[d] for d in range(mine)]
        squares = [product(x, x, first) for x in values]
        for d in range(mine):
            x = values[d]
            iterate[d] = 1.5 * x - 0.5 * product(x, squares[d], second)

    def run(plan):
        at = 0
        while at < len(plan):
            length = 1
            while at + length < len(plan) and plan[at + length] == plan[at]:
                length += 1
            passes = plan[at]

            def body(i, carry):
                step(passes)
                return carry

            lax.fori_loop(0, length, body, 0)
            at += length

    def finish(d):
        (live_row, live_column), count = live(d)
        return 0.5 * (iterate[d] + jnp.where(eye, live_row, 0.0)), count

    fetch.wait()
    for d in range(mine):
        field = load_field(field_ref, fbuf.at[d], d, mine, width)
        potential = product(mapping_t, product(field, mapping, 3), 3)
        value = load_square(core_buf, low.at[d], high.at[d], d, mine, full) + potential
        value = 0.5 * (value + value.T)
        fock[d] = value
        begin(value, d)
    for d in range(mine):
        store_square(section_ref.at[0], fock[d], low.at[d], high.at[d], d, mine, full)
    run(FIRST_PLAN)
    for d in range(mine):
        density, count = finish(d)
        occupied = jnp.sum(jnp.where(eye, density, 0.0), axis=1, keepdims=True)
        coulomb = jnp.sum(symmetric * occupied, axis=0, keepdims=True)
        change = jnp.where(eye, coulomb, 0.0) - 0.5 * symmetric * density
        core_fock = fock[d]
        begin(core_fock + change, d)
        fock[d] = 2.0 * core_fock + change
    run(LAST_PLAN)
    energy = jnp.zeros((1, 1), jnp.float32)
    for d in range(mine):
        density, count = finish(d)
        energy = energy + 0.5 * total(density * fock[d]) / count
        store_square(section_ref.at[1], density, low.at[d], high.at[d], d, mine, full)
    energy_ref[...] = jnp.broadcast_to(energy, energy_ref.shape)


def solve(groups, field, sizes, pairs, core, mapping, repulsion):
    width, full = mapping.shape
    mine = pairs.shape[1] // groups // 2
    tiles = full * full // LANES
    vmem = pl.BlockSpec(memory_space=pltpu.VMEM)
    return pl.pallas_call(
        functools.partial(solve_kernel, groups),
        out_shape=(
            jax.ShapeDtypeStruct((2, tiles * mine, LANES), jnp.float32),
            jax.ShapeDtypeStruct((8, LANES), jnp.float32),
        ),
        in_specs=[vmem, vmem, vmem, pl.BlockSpec(memory_space=pl.ANY), vmem, vmem],
        out_specs=(vmem, vmem),
        scratch_shapes=[
            pltpu.VMEM((tiles * mine, LANES), jnp.float32),
            pltpu.VMEM((mine, full, LANES), jnp.float32),
            pltpu.VMEM((mine, full, LANES), jnp.float32),
            pltpu.VMEM((mine, width, LANES), jnp.float32),
            pltpu.VMEM((mine, full, full), jnp.float32),
            pltpu.VMEM((mine, full, full), jnp.float32),
            pltpu.SemaphoreType.DMA,
        ],
    )(field, sizes, pairs, core, mapping, repulsion)


def share_kernel(groups, energy_ref, section_ref, total_ref, out_ref, gathered, send_sem, recv_sem, part_send, part_recv, own_sem):
    me = lax.axis_index("grp")
    seg = lax.axis_index("segment")
    count = 2 * groups
    index = seg * groups + me
    barrier = pltpu.get_barrier_semaphore()

    def place(offset):
        other = lax.rem(index + offset, count)
        return other // groups, lax.rem(other, groups)

    for offset in range(1, count):
        pl.semaphore_signal(barrier, inc=1, device_id=place(offset), device_id_type=MESH)
    keep = pltpu.make_async_copy(section_ref.at[seg], out_ref.at[seg], own_sem)
    keep.start()
    pl.semaphore_wait(barrier, count - 1)
    give = pltpu.make_async_remote_copy(
        src_ref=section_ref.at[1 - seg], dst_ref=out_ref.at[seg], send_sem=part_send, recv_sem=part_recv,
        device_id=(1 - seg, me), device_id_type=MESH,
    )
    give.start()
    copies = []
    for offset in range(1, count):
        copy = pltpu.make_async_remote_copy(
            src_ref=energy_ref, dst_ref=gathered.at[index], send_sem=send_sem.at[offset], recv_sem=recv_sem.at[offset],
            device_id=place(offset), device_id_type=MESH,
        )
        copy.start()
        copies.append(copy)
    gathered[index] = energy_ref[...]
    for copy in copies:
        copy.wait()
    total_ref[...] = jnp.sum(gathered[...], axis=0)
    keep.wait()
    give.wait()


def share(groups, energy, section):
    count = 2 * groups
    anywhere = pl.BlockSpec(memory_space=pl.ANY)
    vmem = pl.BlockSpec(memory_space=pltpu.VMEM)
    return pl.pallas_call(
        functools.partial(share_kernel, groups),
        out_shape=(
            jax.ShapeDtypeStruct(energy.shape, jnp.float32),
            jax.ShapeDtypeStruct(section.shape, jnp.float32),
        ),
        in_specs=[vmem, vmem],
        out_specs=(vmem, vmem),
        scratch_shapes=[
            pltpu.VMEM((count,) + energy.shape, jnp.float32),
            pltpu.SemaphoreType.DMA((count,)),
            pltpu.SemaphoreType.DMA((count,)),
            pltpu.SemaphoreType.DMA,
            pltpu.SemaphoreType.DMA,
            pltpu.SemaphoreType.DMA,
        ],
        compiler_params=pltpu.CompilerParams(collective_id=1, has_side_effects=True),
    )(energy, section)


def on_device(groups, monomer_density, monomer_centers, dimer_pairs, basis_sizes, dimer_core, esp_map, repulsion):
    dims, flat = dimer_core.shape
    mine = dims // 2
    tiles = flat // LANES
    core = dimer_core.reshape(2, mine, tiles, LANES).transpose(0, 2, 1, 3).reshape(2, tiles * mine, LANES)
    field = make_field(groups, monomer_density, monomer_centers, dimer_pairs)
    field = field.reshape(-1, LANES)
    section, energy = solve(
        groups, field, basis_sizes.reshape(1, -1), dimer_pairs, core, esp_map, repulsion.reshape(tiles, LANES)
    )
    total, section = share(groups, energy, section)
    section = section.reshape(2, tiles, mine, LANES).transpose(0, 2, 1, 3).reshape(1, dims, flat)
    return section, total[0, 0] / dimer_pairs.shape[1]


def solution(mesh):
    in_specs = (P("grp", None), P(), P(), P(), P("grp", None), P(), P())
    out_specs = (P("segment", "grp", None), P())
    return jax.shard_map(
        functools.partial(on_device, mesh.shape["grp"]), mesh=mesh, in_specs=in_specs, out_specs=out_specs, check_vma=False
    )
```

```python
import functools

import jax
import jax.numpy as jnp
from jax import lax
from jax.experimental import pallas as pl
from jax.experimental.pallas import tpu as pltpu
from jax.sharding import PartitionSpec as P

PURIFY = 8
epsilon = 1e-06
LANES = 128
SPLITS = 2
KEEP = pltpu.VMEM
MESH = pl.DeviceIdType.MESH
FIRST_PLAN = ((1, 1),) * PURIFY
LAST_PLAN = ((1, 1),) * (PURIFY - 3) + ((3, 3),) * 3


def flow_orders(groups):
    top, *rest = reversed([1 << k for k in range(groups.bit_length() - 1)])
    orders = [[top] + rest[f * len(rest) // 3:] + rest[:f * len(rest) // 3] for f in range(3)]
    return orders * SPLITS


def bf(value):
    return value.astype(jnp.bfloat16)


def dot(left, right):
    return jnp.dot(left, right, preferred_element_type=jnp.float32)


def split(value):
    high = bf(value)
    return high, bf(value - high.astype(jnp.float32))


def product(left, right, passes):
    if passes == 1:
        return dot(bf(left), bf(right))
    left_high, left_low = split(left)
    right_high, right_low = split(right)
    return dot(left_high, right_high) + (dot(left_high, right_low) + dot(left_low, right_high))


def iota(shape, axis):
    return lax.broadcasted_iota(jnp.int32, shape, axis)


def pair_ids(pairs_ref, positions):
    count = positions.shape[0]
    hit = iota((count, pairs_ref.shape[1]), 1) == positions
    out = []
    for side in range(2):
        row = pairs_ref[side:side + 1, :].astype(jnp.float32)
        out.append(jnp.sum(jnp.where(hit, row, 0.0), axis=1, keepdims=True).astype(jnp.int32))
    return out


def rolled(value, shift):
    return pltpu.roll(value, shift, 1)


def load_field(field_ref, buffer, d, width):
    count = width * width // LANES // 3
    a, b, c = [field_ref[pl.ds(j, count, stride=3), d, :] for j in range(3)]
    lane = iota((count, LANES), 1)
    buffer[pl.ds(0, count, stride=4), :] = a
    buffer[pl.ds(1, count, stride=4), :] = jnp.where(lane < 32, rolled(a, 32), rolled(b, 32))
    buffer[pl.ds(2, count, stride=4), :] = jnp.where(lane < 64, rolled(b, 64), rolled(c, 64))
    buffer[pl.ds(3, count, stride=4), :] = rolled(c, 96)
    return buffer[:, :width]


def load_square(source, low, high, d, mine, full):
    count = full // 2
    a, b, c = [source[pl.ds(j * mine + d, count, stride=3 * mine), :] for j in range(3)]
    lane = iota((count, LANES), 1)
    shifted = rolled(c, 64)
    low[pl.ds(0, count, stride=2), :] = a
    high[pl.ds(0, count, stride=2), :] = b
    low[pl.ds(1, count, stride=2), :] = jnp.where(lane < 64, rolled(b, 64), shifted)
    high[pl.ds(1, count, stride=2), :] = shifted
    return jnp.concatenate([low[...], high[:, :full - LANES]], axis=1)


def store_square(target, value, low, high, full):
    count = full // 2
    low[...] = value[:, :LANES]
    high[:, :full - LANES] = value[:, LANES:]
    lane = iota((count, LANES), 1)
    even_low = low[pl.ds(0, count, stride=2), :]
    even_high = high[pl.ds(0, count, stride=2), :]
    odd_low = rolled(low[pl.ds(1, count, stride=2), :], 64)
    odd_high = rolled(high[pl.ds(1, count, stride=2), :], 64)
    pieces = (even_low, jnp.where(lane < 64, even_high, odd_low), jnp.where(lane < 64, odd_low, odd_high))
    for j, piece in enumerate(pieces):
        target[pl.ds(j, count, stride=3), :] = piece


def solve_kernel(
    groups, density_ref, centers_ref, pairs_ref, sizes_ref, core_ref, map_ref, rep_ref,
    stage_ref, arrived_ref, gathered,
    blocks, given, field_ref, core_buf, low, high, fbuf, fock, iterate, energy_ref,
    send_sem, recv_sem, own_sem, part_send, part_recv, sum_send, sum_recv, section_send, section_recv, core_sem,
):
    me = lax.axis_index("grp")
    seg = lax.axis_index("segment")
    rows, flat = density_ref.shape
    orders = flow_orders(groups)
    flows = len(orders)
    stages = len(orders[0])
    half = flat // 2
    columns = half // flows
    tiles = half // LANES
    each = columns // LANES
    monomers = centers_ref.shape[1]
    width, full = map_ref.shape
    dims = pairs_ref.shape[1] // groups
    mine = dims // 2
    devices = 2 * groups
    index = seg * groups + me

    def place_of(offset):
        other = lax.rem(index + offset, devices)
        return other // groups, lax.rem(other, groups)

    barrier = pltpu.get_barrier_semaphore()
    for offset in range(1, devices):
        pl.semaphore_signal(barrier, inc=1, device_id=place_of(offset), device_id_type=MESH)
    own = []
    for f in range(flows):
        start = pl.multiple_of(seg * half + f * columns, LANES)
        source = density_ref.at[:, pl.ds(start, columns)]
        copy = pltpu.make_async_copy(source, blocks.at[f, 0], own_sem.at[f])
        copy.start()
        own.append(copy)
    fetch = pltpu.make_async_copy(core_ref.at[seg], core_buf, core_sem)
    fetch.start()
    pl.semaphore_wait(barrier, devices - 1)

    def exchange(f, k):
        count = 1 << k
        return pltpu.make_async_remote_copy(
            src_ref=blocks.at[f, pl.ds(0, count)],
            dst_ref=blocks.at[f, pl.ds(count, count)],
            send_sem=send_sem.at[f, k],
            recv_sem=recv_sem.at[f, k],
            device_id=(seg, me ^ orders[f][k]),
            device_id_type=MESH,
        )

    for f in range(flows):
        own[f].wait()
        exchange(f, 0).start()

    place = iota((dims, 1), 0)
    positions = me * dims + jnp.where(place < mine, seg * mine + place, (1 - seg) * mine + place - mine)
    ids = pair_ids(pairs_ref, positions)
    labels = iota((dims, monomers), 1)
    is_first, is_second = [labels == i for i in ids]
    distance = jnp.zeros((dims, monomers), jnp.float32)
    for axis in range(centers_ref.shape[0]):
        row = centers_ref[axis:axis + 1, :]
        first_at = jnp.sum(jnp.where(is_first, row, 0.0), axis=1, keepdims=True)
        second_at = jnp.sum(jnp.where(is_second, row, 0.0), axis=1, keepdims=True)
        gap = 0.5 * (first_at + second_at) - row
        distance = distance + gap * gap
    weights = bf(jnp.where(is_first | is_second, 0.0, 1.0 / jnp.sqrt(distance + 1.0)))
    ordered = []
    for f in range(flows // SPLITS):
        column = iota((monomers, monomers), 1)
        slot = column // rows
        owner = jnp.full_like(column, me)
        for k, bit in enumerate(orders[f]):
            owner = owner ^ jnp.where((slot & (1 << k)) != 0, bit, 0)
        label = owner * rows + (column & (rows - 1))
        chosen = bf(jnp.where(iota((monomers, monomers), 0) == label, 1.0, 0.0))
        ordered.append(bf(dot(weights, chosen)))
    sizes = [
        jnp.sum(jnp.where(hit, sizes_ref[...].astype(jnp.float32), 0.0), axis=1, keepdims=True)[:mine]
        for hit in (is_first, is_second)
    ]

    for k in range(1, stages):
        for f in range(flows):
            exchange(f, k - 1).wait_recv()
            exchange(f, k).start()

    row_at = iota((1, full), 1)
    column_at = iota((full, 1), 0)
    eye = iota((full, full), 0) == iota((full, full), 1)
    repulsion = load_square(rep_ref, low.at[0], high.at[0], 0, 1, full)
    symmetric = 0.5 * (repulsion + repulsion.T)
    mapping = map_ref[...]
    mapping_t = mapping.T
    fetch.wait()
    for d in range(mine):
        value = load_square(core_buf, low.at[d], high.at[d], d, mine, full)
        fock[d] = 0.5 * (value + value.T)

    def partial(f, first, count):
        block = bf(blocks[f, first:first + count].astype(jnp.float32).reshape(count * rows, columns))
        return dot(ordered[f % (flows // SPLITS)][:, first * rows:(first + count) * rows], block)

    early = [partial(f, 0, groups // 2) for f in range(flows)]

    def give(f):
        return pltpu.make_async_remote_copy(
            src_ref=given.at[pl.ds(f * each, each)],
            dst_ref=field_ref.at[pl.ds(seg * tiles + f * each, each)],
            send_sem=part_send.at[f], recv_sem=part_recv.at[f],
            device_id=(1 - seg, me), device_id_type=MESH,
        )

    for f in range(flows):
        exchange(f, stages - 1).wait_recv()
        result = early[f] + partial(f, groups // 2, groups // 2)
        for t in range(each):
            piece = result[:, t * LANES:(t + 1) * LANES]
            field_ref[seg * tiles + f * each + t] = piece[:mine]
            given[f * each + t] = piece[mine:]
        give(f).start()
    for f in range(flows):
        for k in range(stages):
            exchange(f, k).wait_send()
    for f in range(flows):
        give(f).wait()

    def live(d):
        first, second = [s[d:d + 1, :] for s in sizes]
        out = []
        for at in (row_at, column_at):
            limit = jnp.where(at < width, first, second + width)
            out.append(jnp.where(at.astype(jnp.float32) < limit, 1.0, 0.0))
        return out, first + second

    def total(value):
        return jnp.sum(jnp.sum(value, axis=0, keepdims=True), axis=1, keepdims=True)

    def begin(matrix, d):
        (live_row, live_column), count = live(d)
        masked = matrix * (live_column * live_row)
        chemical = total(jnp.where(eye, masked, 0.0)) / count
        shifted = masked - jnp.where(eye, chemical * live_row, 0.0)
        radius = jnp.max(jnp.sum(jnp.abs(shifted), axis=0, keepdims=True), axis=1, keepdims=True)
        iterate[d] = shifted * (-1.0 / (radius + epsilon))

    def step(passes):
        first, second = passes
        values = [iterate[d] for d in range(mine)]
        squares = [product(x, x, first) for x in values]
        for d in range(mine):
            x = values[d]
            iterate[d] = 1.5 * x - 0.5 * product(x, squares[d], second)

    def run(plan):
        at = 0
        while at < len(plan):
            length = 1
            while at + length < len(plan) and plan[at + length] == plan[at]:
                length += 1
            passes = plan[at]

            def body(i, carry):
                step(passes)
                return carry

            lax.fori_loop(0, length, body, 0)
            at += length

    def finish(d):
        (live_row, live_column), count = live(d)
        return 0.5 * (iterate[d] + jnp.where(eye, live_row, 0.0)), count

    def swap(part, d):
        return pltpu.make_async_remote_copy(
            src_ref=stage_ref.at[part, d], dst_ref=arrived_ref.at[d],
            send_sem=section_send.at[d], recv_sem=section_recv.at[d],
            device_id=(1 - seg, me), device_id_type=MESH,
        )

    for d in range(mine):
        field = load_field(field_ref, fbuf.at[d], d, width)
        field = 0.5 * (field + field.T)
        value = fock[d] + product(mapping_t, product(field, mapping, 3), 3)
        fock[d] = value
        begin(value, d)
    for d in range(mine):
        store_square(stage_ref.at[0, d], fock[d], low.at[d], high.at[d], full)

    @pl.when(seg == 1)
    def _():
        for d in range(mine):
            swap(0, d).start()

    run(FIRST_PLAN)
    for d in range(mine):
        density, count = finish(d)
        occupied = jnp.sum(jnp.where(eye, density, 0.0), axis=1, keepdims=True)
        coulomb = jnp.sum(symmetric * occupied, axis=0, keepdims=True)
        change = jnp.where(eye, coulomb, 0.0) - 0.5 * symmetric * density
        core_fock = fock[d]
        begin(core_fock + change, d)
        fock[d] = 2.0 * core_fock + change
    run(LAST_PLAN)
    energy = jnp.zeros((1, 1), jnp.float32)
    for d in range(mine):
        density, count = finish(d)
        energy = energy + 0.5 * total(density * fock[d]) / count
        store_square(stage_ref.at[1, d], density, low.at[d], high.at[d], full)

        @pl.when(seg == 0)
        def _():
            swap(1, d).start()

    energy_ref[...] = jnp.broadcast_to(energy, energy_ref.shape)
    gathered[index] = energy_ref[...]
    copies = []
    for offset in range(1, devices):
        copy = pltpu.make_async_remote_copy(
            src_ref=energy_ref, dst_ref=gathered.at[index], send_sem=sum_send.at[offset], recv_sem=sum_recv.at[offset],
            device_id=place_of(offset), device_id_type=MESH,
        )
        copy.start()
        copies.append(copy)
    for copy in copies:
        copy.wait()
    for d in range(mine):
        swap(1 - seg, d).wait()


def solve(groups, density, centers, pairs, sizes, core, mapping, repulsion):
    rows, total = density.shape
    flows = len(flow_orders(groups))
    stages = groups.bit_length() - 1
    half = total // 2
    devices = 2 * groups
    width, full = mapping.shape
    mine = pairs.shape[1] // groups // 2
    tiles = full * full // LANES
    vmem = pl.BlockSpec(memory_space=pltpu.VMEM)
    anywhere = pl.BlockSpec(memory_space=pl.ANY)
    return pl.pallas_call(
        functools.partial(solve_kernel, groups),
        out_shape=(
            KEEP((2, mine, tiles, LANES), jnp.float32),
            KEEP((mine, tiles, LANES), jnp.float32),
            KEEP((devices, 1, LANES), jnp.float32),
        ),
        in_specs=[anywhere, vmem, vmem, vmem, anywhere, vmem, vmem],
        out_specs=(vmem, vmem, vmem),
        scratch_shapes=[
            pltpu.VMEM((flows, groups, rows, half // flows), jnp.bfloat16),
            pltpu.VMEM((half // LANES, mine, LANES), jnp.float32),
            pltpu.VMEM((total // LANES, mine, LANES), jnp.float32),
            pltpu.VMEM((tiles * mine, LANES), jnp.float32),
            pltpu.VMEM((mine, full, LANES), jnp.float32),
            pltpu.VMEM((mine, full, LANES), jnp.float32),
            pltpu.VMEM((mine, width, LANES), jnp.float32),
            pltpu.VMEM((mine, full, full), jnp.float32),
            pltpu.VMEM((mine, full, full), jnp.float32),
            pltpu.VMEM((1, LANES), jnp.float32),
            pltpu.SemaphoreType.DMA((flows, stages)),
            pltpu.SemaphoreType.DMA((flows, stages)),
            pltpu.SemaphoreType.DMA((flows,)),
            pltpu.SemaphoreType.DMA((flows,)),
            pltpu.SemaphoreType.DMA((flows,)),
            pltpu.SemaphoreType.DMA((devices,)),
            pltpu.SemaphoreType.DMA((devices,)),
            pltpu.SemaphoreType.DMA((mine,)),
            pltpu.SemaphoreType.DMA((mine,)),
            pltpu.SemaphoreType.DMA,
        ],
        compiler_params=pltpu.CompilerParams(collective_id=0, has_side_effects=True, vmem_limit_bytes=40 << 20),
    )(density, centers, pairs, sizes, core, mapping, repulsion)


def merge_kernel(share, stage_ref, arrived_ref, gathered, out_ref, total_ref):
    seg = lax.axis_index("segment")
    half = pl.program_id(0)
    mine, tiles, _ = arrived_ref.shape

    @pl.when(half == 0)
    def _():
        total_ref[...] = jnp.sum(gathered[...], axis=0)[:, :1] * share

    @pl.when(half == seg)
    def _():
        for d in range(mine):
            out_ref[0, pl.ds(d, tiles, stride=mine), :] = stage_ref[seg, d]

    @pl.when(half != seg)
    def _():
        for d in range(mine):
            out_ref[0, pl.ds(d, tiles, stride=mine), :] = arrived_ref[d]


def merge(share, stage, arrived, gathered):
    mine, tiles, _ = arrived.shape
    vmem = pl.BlockSpec(memory_space=pltpu.VMEM)
    return pl.pallas_call(
        functools.partial(merge_kernel, share),
        out_shape=(
            jax.ShapeDtypeStruct((2, tiles * mine, LANES), jnp.float32),
            jax.ShapeDtypeStruct((1, 1), jnp.float32),
        ),
        grid=(2,),
        in_specs=[vmem, vmem, vmem],
        out_specs=(
            pl.BlockSpec((1, tiles * mine, LANES), lambda i: (i, 0, 0)),
            pl.BlockSpec((1, 1), lambda i: (0, 0)),
        ),
        compiler_params=pltpu.CompilerParams(vmem_limit_bytes=16 << 20),
    )(stage, arrived, gathered)


def on_device(groups, monomer_density, monomer_centers, dimer_pairs, basis_sizes, dimer_core, esp_map, repulsion):
    dims, flat = dimer_core.shape
    mine = dims // 2
    tiles = flat // LANES
    core = dimer_core.reshape(2, mine, tiles, LANES).transpose(0, 2, 1, 3).reshape(2, tiles * mine, LANES)
    stage, arrived, gathered = solve(
        groups, monomer_density, monomer_centers, dimer_pairs, basis_sizes.reshape(1, -1), core, esp_map,
        repulsion.reshape(tiles, LANES),
    )
    section, total = merge(1.0 / dimer_pairs.shape[1], stage, arrived, gathered)
    section = section.reshape(2, tiles, mine, LANES).transpose(0, 2, 1, 3).reshape(1, dims, flat)
    return section, total[0, 0]


def solution(mesh):
    in_specs = (P("grp", None), P(), P(), P(), P("grp", None), P(), P())
    out_specs = (P("segment", "grp", None), P())
    return jax.shard_map(
        functools.partial(on_device, mesh.shape["grp"]), mesh=mesh, in_specs=in_specs, out_specs=out_specs, check_vma=False
    )
```

```python
import functools

import jax
import jax.numpy as jnp
from jax import lax
from jax.experimental import pallas as pl
from jax.experimental.pallas import tpu as pltpu
from jax.sharding import PartitionSpec as P

PURIFY = 8
epsilon = 1e-06
LANES = 128
SPLITS = 3
KEEP = pltpu.VMEM
MESH = pl.DeviceIdType.MESH
FIRST_PLAN = ((1, 1),) * PURIFY
LAST_PLAN = ((1, 1),) * (PURIFY - 3) + ((3, 3),) * 3


def flow_orders(groups):
    top, *rest = reversed([1 << k for k in range(groups.bit_length() - 1)])
    orders = [[top] + rest[f * len(rest) // 3:] + rest[:f * len(rest) // 3] for f in range(3)]
    return orders * SPLITS


def bf(value):
    return value.astype(jnp.bfloat16)


def dot(left, right):
    return jnp.dot(left, right, preferred_element_type=jnp.float32)


def split(value):
    high = bf(value)
    return high, bf(value - high.astype(jnp.float32))


def product(left, right, passes):
    if passes == 1:
        return dot(bf(left), bf(right))
    left_high, left_low = split(left)
    right_high, right_low = split(right)
    return dot(left_high, right_high) + (dot(left_high, right_low) + dot(left_low, right_high))


def iota(shape, axis):
    return lax.broadcasted_iota(jnp.int32, shape, axis)


def pair_ids(pairs_ref, positions):
    count = positions.shape[0]
    hit = iota((count, pairs_ref.shape[1]), 1) == positions
    out = []
    for side in range(2):
        row = pairs_ref[side:side + 1, :].astype(jnp.float32)
        out.append(jnp.sum(jnp.where(hit, row, 0.0), axis=1, keepdims=True).astype(jnp.int32))
    return out


def rolled(value, shift):
    return pltpu.roll(value, shift, 1)


def load_field(field_ref, buffer, d, width):
    count = width * width // LANES // 3
    a, b, c = [field_ref[pl.ds(j, count, stride=3), d, :] for j in range(3)]
    lane = iota((count, LANES), 1)
    buffer[pl.ds(0, count, stride=4), :] = a
    buffer[pl.ds(1, count, stride=4), :] = jnp.where(lane < 32, rolled(a, 32), rolled(b, 32))
    buffer[pl.ds(2, count, stride=4), :] = jnp.where(lane < 64, rolled(b, 64), rolled(c, 64))
    buffer[pl.ds(3, count, stride=4), :] = rolled(c, 96)
    return buffer[:, :width]


def load_square(source, low, high, d, mine, full):
    count = full // 2
    a, b, c = [source[pl.ds(j * mine + d, count, stride=3 * mine), :] for j in range(3)]
    lane = iota((count, LANES), 1)
    shifted = rolled(c, 64)
    low[pl.ds(0, count, stride=2), :] = a
    high[pl.ds(0, count, stride=2), :] = b
    low[pl.ds(1, count, stride=2), :] = jnp.where(lane < 64, rolled(b, 64), shifted)
    high[pl.ds(1, count, stride=2), :] = shifted
    return jnp.concatenate([low[...], high[:, :full - LANES]], axis=1)


def store_square(target, value, low, high, full):
    count = full // 2
    low[...] = value[:, :LANES]
    high[:, :full - LANES] = value[:, LANES:]
    lane = iota((count, LANES), 1)
    even_low = low[pl.ds(0, count, stride=2), :]
    even_high = high[pl.ds(0, count, stride=2), :]
    odd_low = rolled(low[pl.ds(1, count, stride=2), :], 64)
    odd_high = rolled(high[pl.ds(1, count, stride=2), :], 64)
    pieces = (even_low, jnp.where(lane < 64, even_high, odd_low), jnp.where(lane < 64, odd_low, odd_high))
    for j, piece in enumerate(pieces):
        target[pl.ds(j, count, stride=3), :] = piece


def solve_kernel(
    groups, density_ref, centers_hbm, pairs_hbm, sizes_hbm, core_ref, map_hbm, rep_hbm,
    stage_ref, arrived_ref, total_ref,
    gathered, blocks, given, field_ref, core_buf, low, high, fbuf, fock, iterate, energy_ref,
    send_sem, recv_sem, own_sem, part_send, part_recv, sum_send, sum_recv, section_send, section_recv, core_sem,
    centers_ref, pairs_ref, sizes_ref, map_ref, rep_ref, small_sem,
):
    me = lax.axis_index("grp")
    seg = lax.axis_index("segment")
    rows, flat = density_ref.shape
    orders = flow_orders(groups)
    flows = len(orders)
    stages = len(orders[0])
    half = flat // 2
    columns = half // flows
    tiles = half // LANES
    each = columns // LANES
    monomers = centers_ref.shape[1]
    width, full = map_ref.shape
    dims = pairs_ref.shape[1] // groups
    mine = dims // 2
    devices = 2 * groups
    index = seg * groups + me

    def place_of(offset):
        other = lax.rem(index + offset, devices)
        return other // groups, lax.rem(other, groups)

    barrier = pltpu.get_barrier_semaphore()
    for bit in sorted(orders[0]):
        pl.semaphore_signal(barrier, inc=1, device_id=(seg, me ^ bit), device_id_type=MESH)
    pl.semaphore_signal(barrier, inc=1, device_id=(1 - seg, me), device_id_type=MESH)
    own = []
    for f in range(flows):
        start = pl.multiple_of(seg * half + f * columns, LANES)
        source = density_ref.at[:, pl.ds(start, columns)]
        copy = pltpu.make_async_copy(source, blocks.at[f, 0], own_sem.at[f])
        copy.start()
        own.append(copy)
    fetch = pltpu.make_async_copy(core_ref.at[seg], core_buf, core_sem)
    fetch.start()
    small = []
    for i, (source, target) in enumerate((
        (centers_hbm, centers_ref), (pairs_hbm, pairs_ref), (sizes_hbm, sizes_ref), (map_hbm, map_ref), (rep_hbm, rep_ref),
    )):
        copy = pltpu.make_async_copy(source, target, small_sem.at[i])
        copy.start()
        small.append(copy)
    pl.semaphore_wait(barrier, stages + 1)

    def exchange(f, k):
        count = 1 << k
        return pltpu.make_async_remote_copy(
            src_ref=blocks.at[f, pl.ds(0, count)],
            dst_ref=blocks.at[f, pl.ds(count, count)],
            send_sem=send_sem.at[f, k],
            recv_sem=recv_sem.at[f, k],
            device_id=(seg, me ^ orders[f][k]),
            device_id_type=MESH,
        )

    for f in range(flows):
        own[f].wait()
        exchange(f, 0).start()

    for copy in small:
        copy.wait()

    place = iota((dims, 1), 0)
    positions = me * dims + jnp.where(place < mine, seg * mine + place, (1 - seg) * mine + place - mine)
    ids = pair_ids(pairs_ref, positions)
    labels = iota((dims, monomers), 1)
    is_first, is_second = [labels == i for i in ids]
    distance = jnp.zeros((dims, monomers), jnp.float32)
    for axis in range(centers_ref.shape[0]):
        row = centers_ref[axis:axis + 1, :]
        first_at = jnp.sum(jnp.where(is_first, row, 0.0), axis=1, keepdims=True)
        second_at = jnp.sum(jnp.where(is_second, row, 0.0), axis=1, keepdims=True)
        gap = 0.5 * (first_at + second_at) - row
        distance = distance + gap * gap
    weights = bf(jnp.where(is_first | is_second, 0.0, 1.0 / jnp.sqrt(distance + 1.0)))
    ordered = []
    for f in range(flows // SPLITS):
        column = iota((monomers, monomers), 1)
        slot = column // rows
        owner = jnp.full_like(column, me)
        for k, bit in enumerate(orders[f]):
            owner = owner ^ jnp.where((slot & (1 << k)) != 0, bit, 0)
        label = owner * rows + (column & (rows - 1))
        chosen = bf(jnp.where(iota((monomers, monomers), 0) == label, 1.0, 0.0))
        ordered.append(bf(dot(weights, chosen)))
    sizes = [
        jnp.sum(jnp.where(hit, sizes_ref[...].astype(jnp.float32), 0.0), axis=1, keepdims=True)[:mine]
        for hit in (is_first, is_second)
    ]

    for k in range(1, stages):
        for f in range(flows):
            exchange(f, k - 1).wait_recv()
            exchange(f, k).start()

    row_at = iota((1, full), 1)
    column_at = iota((full, 1), 0)
    eye = iota((full, full), 0) == iota((full, full), 1)
    repulsion = load_square(rep_ref, low.at[0], high.at[0], 0, 1, full)
    symmetric = 0.5 * (repulsion + repulsion.T)
    mapping = map_ref[...]
    mapping_t = mapping.T
    fetch.wait()
    for d in range(mine):
        value = load_square(core_buf, low.at[d], high.at[d], d, mine, full)
        fock[d] = 0.5 * (value + value.T)

    def partial(f, first, count):
        block = bf(blocks[f, first:first + count].astype(jnp.float32).reshape(count * rows, columns))
        return dot(ordered[f % (flows // SPLITS)][:, first * rows:(first + count) * rows], block)

    early = [partial(f, 0, groups // 2) for f in range(flows)]

    def give(f):
        return pltpu.make_async_remote_copy(
            src_ref=given.at[pl.ds(f * each, each)],
            dst_ref=field_ref.at[pl.ds(seg * tiles + f * each, each)],
            send_sem=part_send.at[f], recv_sem=part_recv.at[f],
            device_id=(1 - seg, me), device_id_type=MESH,
        )

    for f in range(flows):
        exchange(f, stages - 1).wait_recv()
        result = early[f] + partial(f, groups // 2, groups // 2)
        for t in range(each):
            piece = result[:, t * LANES:(t + 1) * LANES]
            field_ref[seg * tiles + f * each + t] = piece[:mine]
            given[f * each + t] = piece[mine:]
        give(f).start()
    for f in range(flows):
        for k in range(stages):
            exchange(f, k).wait_send()
    for f in range(flows):
        give(f).wait()

    def live(d):
        first, second = [s[d:d + 1, :] for s in sizes]
        out = []
        for at in (row_at, column_at):
            limit = jnp.where(at < width, first, second + width)
            out.append(jnp.where(at.astype(jnp.float32) < limit, 1.0, 0.0))
        return out, first + second

    def begin_all(matrices):
        masks = [live(d) for d in range(mine)]
        for d in range(mine):
            (live_row, live_column), count = masks[d]
            iterate[d] = matrices[d]() * (live_column * live_row)
        traces = [jnp.sum(jnp.where(eye, iterate[d], 0.0), axis=0, keepdims=True) for d in range(mine)]
        levels = [jnp.sum(t, axis=1, keepdims=True) / masks[d][1] for d, t in enumerate(traces)]
        sums = []
        for d in range(mine):
            shifted = iterate[d] - jnp.where(eye, levels[d] * masks[d][0][0], 0.0)
            iterate[d] = shifted
            sums.append(jnp.sum(jnp.abs(shifted), axis=0, keepdims=True))
        scales = [-1.0 / (jnp.max(t, axis=1, keepdims=True) + epsilon) for t in sums]
        for d in range(mine):
            iterate[d] = iterate[d] * scales[d]

    def step(passes):
        first, second = passes
        values = [iterate[d] for d in range(mine)]
        squares = [product(x, x, first) for x in values]
        for d in range(mine):
            x = values[d]
            iterate[d] = 1.5 * x - 0.5 * product(x, squares[d], second)

    def run(plan):
        at = 0
        while at < len(plan):
            length = 1
            while at + length < len(plan) and plan[at + length] == plan[at]:
                length += 1
            passes = plan[at]

            def body(i, carry):
                step(passes)
                return carry

            lax.fori_loop(0, length, body, 0)
            at += length

    def finish(d):
        (live_row, live_column), count = live(d)
        return 0.5 * (iterate[d] + jnp.where(eye, live_row, 0.0)), count

    def swap(part, d):
        return pltpu.make_async_remote_copy(
            src_ref=stage_ref.at[part, d], dst_ref=arrived_ref.at[d],
            send_sem=section_send.at[d], recv_sem=section_recv.at[d],
            device_id=(1 - seg, me), device_id_type=MESH,
        )

    fields = [load_field(field_ref, fbuf.at[d], d, width) for d in range(mine)]
    fields = [0.5 * (field + field.T) for field in fields]
    lefts = [product(field, mapping, 3) for field in fields]
    for d in range(mine):
        fock[d] = fock[d] + product(mapping_t, lefts[d], 3)
    begin_all([lambda d=d: fock[d] for d in range(mine)])
    for d in range(mine):
        store_square(stage_ref.at[0, d], fock[d], low.at[d], high.at[d], full)

    @pl.when(seg == 1)
    def _():
        for d in range(mine):
            swap(0, d).start()

    run(FIRST_PLAN)
    def rebuilt(d):
        density, count = finish(d)
        occupied = jnp.sum(jnp.where(eye, density, 0.0), axis=1, keepdims=True)
        coulomb = jnp.sum(symmetric * occupied, axis=0, keepdims=True)
        change = jnp.where(eye, coulomb, 0.0) - 0.5 * symmetric * density
        core_fock = fock[d]
        fock[d] = 2.0 * core_fock + change
        return core_fock + change

    begin_all([functools.partial(rebuilt, d) for d in range(mine)])
    run(LAST_PLAN)
    partials = jnp.zeros((1, full), jnp.float32)
    for d in range(mine):
        density, count = finish(d)
        iterate[d] = density
        partials = partials + jnp.sum(density * fock[d], axis=0, keepdims=True) * (0.5 / count)
    energy = jnp.sum(partials, axis=1, keepdims=True)
    energy_ref[...] = jnp.broadcast_to(energy, energy_ref.shape)
    gathered[index] = energy_ref[...]
    copies = []
    for offset in range(1, devices):
        copy = pltpu.make_async_remote_copy(
            src_ref=energy_ref, dst_ref=gathered.at[index], send_sem=sum_send.at[offset], recv_sem=sum_recv.at[offset],
            device_id=place_of(offset), device_id_type=MESH,
        )
        copy.start()
        copies.append(copy)
    for d in range(mine):
        store_square(stage_ref.at[1, d], iterate[d], low.at[d], high.at[d], full)

        @pl.when(seg == 0)
        def _():
            swap(1, d).start()

    for copy in copies:
        copy.wait()
    total_ref[...] = jnp.sum(gathered[...], axis=0)
    for d in range(mine):
        swap(1 - seg, d).wait()


def solve(groups, density, centers, pairs, sizes, core, mapping, repulsion):
    rows, total = density.shape
    flows = len(flow_orders(groups))
    stages = groups.bit_length() - 1
    half = total // 2
    devices = 2 * groups
    width, full = mapping.shape
    mine = pairs.shape[1] // groups // 2
    tiles = full * full // LANES
    vmem = pl.BlockSpec(memory_space=pltpu.VMEM)
    anywhere = pl.BlockSpec(memory_space=pl.ANY)
    return pl.pallas_call(
        functools.partial(solve_kernel, groups),
        out_shape=(
            KEEP((2, mine, tiles, LANES), jnp.float32),
            KEEP((mine, tiles, LANES), jnp.float32),
            KEEP((1, LANES), jnp.float32),
        ),
        in_specs=[anywhere] * 7,
        out_specs=(vmem, vmem, vmem),
        scratch_shapes=[
            pltpu.VMEM((devices, 1, LANES), jnp.float32),
            pltpu.VMEM((flows, groups, rows, half // flows), jnp.bfloat16),
            pltpu.VMEM((half // LANES, mine, LANES), jnp.float32),
            pltpu.VMEM((total // LANES, mine, LANES), jnp.float32),
            pltpu.VMEM((tiles * mine, LANES), jnp.float32),
            pltpu.VMEM((mine, full, LANES), jnp.float32),
            pltpu.VMEM((mine, full, LANES), jnp.float32),
            pltpu.VMEM((mine, width, LANES), jnp.float32),
            pltpu.VMEM((mine, full, full), jnp.float32),
            pltpu.VMEM((mine, full, full), jnp.float32),
            pltpu.VMEM((1, LANES), jnp.float32),
            pltpu.SemaphoreType.DMA((flows, stages)),
            pltpu.SemaphoreType.DMA((flows, stages)),
            pltpu.SemaphoreType.DMA((flows,)),
            pltpu.SemaphoreType.DMA((flows,)),
            pltpu.SemaphoreType.DMA((flows,)),
            pltpu.SemaphoreType.DMA((devices,)),
            pltpu.SemaphoreType.DMA((devices,)),
            pltpu.SemaphoreType.DMA((mine,)),
            pltpu.SemaphoreType.DMA((mine,)),
            pltpu.SemaphoreType.DMA,
            *[pltpu.VMEM(small.shape, small.dtype) for small in (centers, pairs, sizes, mapping, repulsion)],
            pltpu.SemaphoreType.DMA((5,)),
        ],
        compiler_params=pltpu.CompilerParams(collective_id=0, has_side_effects=True),
    )(density, centers, pairs, sizes, core, mapping, repulsion)


def merge_kernel(share, stage_ref, arrived_ref, sum_ref, out_ref, total_ref):
    seg = lax.axis_index("segment")
    half = pl.program_id(0)
    mine, tiles, _ = arrived_ref.shape

    @pl.when(half == 0)
    def _():
        total_ref[...] = sum_ref[:, :1] * share

    @pl.when(half == seg)
    def _():
        for d in range(mine):
            out_ref[0, pl.ds(d, tiles, stride=mine), :] = stage_ref[seg, d]

    @pl.when(half != seg)
    def _():
        for d in range(mine):
            out_ref[0, pl.ds(d, tiles, stride=mine), :] = arrived_ref[d]


def merge(share, stage, arrived, gathered):
    mine, tiles, _ = arrived.shape
    vmem = pl.BlockSpec(memory_space=pltpu.VMEM)
    return pl.pallas_call(
        functools.partial(merge_kernel, share),
        out_shape=(
            jax.ShapeDtypeStruct((2, tiles * mine, LANES), jnp.float32),
            jax.ShapeDtypeStruct((1, 1), jnp.float32),
        ),
        grid=(2,),
        in_specs=[vmem, vmem, vmem],
        out_specs=(
            pl.BlockSpec((1, tiles * mine, LANES), lambda i: (i, 0, 0)),
            pl.BlockSpec((1, 1), lambda i: (0, 0)),
        ),
        compiler_params=pltpu.CompilerParams(vmem_limit_bytes=16 << 20),
    )(stage, arrived, gathered)


def on_device(groups, monomer_density, monomer_centers, dimer_pairs, basis_sizes, dimer_core, esp_map, repulsion):
    dims, flat = dimer_core.shape
    mine = dims // 2
    tiles = flat // LANES
    core = dimer_core.reshape(2, mine, tiles, LANES).transpose(0, 2, 1, 3).reshape(2, tiles * mine, LANES)
    stage, arrived, gathered = solve(
        groups, monomer_density, monomer_centers, dimer_pairs, basis_sizes.reshape(1, -1), core, esp_map,
        repulsion.reshape(tiles, LANES),
    )
    section, total = merge(1.0 / dimer_pairs.shape[1], stage, arrived, gathered)
    section = section.reshape(2, tiles, mine, LANES).transpose(0, 2, 1, 3).reshape(1, dims, flat)
    return section, total[0, 0]


def solution(mesh):
    in_specs = (P("grp", None), P(), P(), P(), P("grp", None), P(), P())
    out_specs = (P("segment", "grp", None), P())
    return jax.shard_map(
        functools.partial(on_device, mesh.shape["grp"]), mesh=mesh, in_specs=in_specs, out_specs=out_specs, check_vma=False
    )
```

```python
import functools

import jax
import jax.numpy as jnp
from jax import lax
from jax.experimental import pallas as pl
from jax.experimental.pallas import tpu as pltpu
from jax.sharding import PartitionSpec as P

PURIFY = 8
epsilon = 1e-06
LANES = 128
SPLITS = 3
KEEP = pltpu.VMEM
MESH = pl.DeviceIdType.MESH
FIRST_PLAN = ((1, 1),) * PURIFY
LAST_PLAN = ((1, 1),) * (PURIFY - 2) + ((3, 3),) * 2


def flow_orders(groups):
    top, *rest = reversed([1 << k for k in range(groups.bit_length() - 1)])
    orders = [[top] + rest[f * len(rest) // 3:] + rest[:f * len(rest) // 3] for f in range(3)]
    return orders * SPLITS


def bf(value):
    return value.astype(jnp.bfloat16)


def dot(left, right):
    return jnp.dot(left, right, preferred_element_type=jnp.float32)


def split(value):
    high = bf(value)
    return high, bf(value - high.astype(jnp.float32))


def product(left, right, passes):
    if passes == 1:
        return dot(bf(left), bf(right))
    left_high, left_low = split(left)
    right_high, right_low = split(right)
    return dot(left_high, right_high) + (dot(left_high, right_low) + dot(left_low, right_high))


def iota(shape, axis):
    return lax.broadcasted_iota(jnp.int32, shape, axis)


def pair_ids(pairs_ref, positions):
    count = positions.shape[0]
    hit = iota((count, pairs_ref.shape[1]), 1) == positions
    out = []
    for side in range(2):
        row = pairs_ref[side:side + 1, :].astype(jnp.float32)
        out.append(jnp.sum(jnp.where(hit, row, 0.0), axis=1, keepdims=True).astype(jnp.int32))
    return out


def rolled(value, shift):
    return pltpu.roll(value, shift, 1)


def load_field(field_ref, buffer, d, width):
    count = width * width // LANES // 3
    a, b, c = [field_ref[pl.ds(j, count, stride=3), d, :] for j in range(3)]
    lane = iota((count, LANES), 1)
    buffer[pl.ds(0, count, stride=4), :] = a
    buffer[pl.ds(1, count, stride=4), :] = jnp.where(lane < 32, rolled(a, 32), rolled(b, 32))
    buffer[pl.ds(2, count, stride=4), :] = jnp.where(lane < 64, rolled(b, 64), rolled(c, 64))
    buffer[pl.ds(3, count, stride=4), :] = rolled(c, 96)
    return buffer[:, :width]


def load_square(source, low, high, d, mine, full):
    count = full // 2
    a, b, c = [source[pl.ds(j * mine + d, count, stride=3 * mine), :] for j in range(3)]
    lane = iota((count, LANES), 1)
    shifted = rolled(c, 64)
    low[pl.ds(0, count, stride=2), :] = a
    high[pl.ds(0, count, stride=2), :] = b
    low[pl.ds(1, count, stride=2), :] = jnp.where(lane < 64, rolled(b, 64), shifted)
    high[pl.ds(1, count, stride=2), :] = shifted
    return jnp.concatenate([low[...], high[:, :full - LANES]], axis=1)


def store_square(target, value, low, high, full):
    count = full // 2
    low[...] = value[:, :LANES]
    high[:, :full - LANES] = value[:, LANES:]
    lane = iota((count, LANES), 1)
    even_low = low[pl.ds(0, count, stride=2), :]
    even_high = high[pl.ds(0, count, stride=2), :]
    odd_low = rolled(low[pl.ds(1, count, stride=2), :], 64)
    odd_high = rolled(high[pl.ds(1, count, stride=2), :], 64)
    pieces = (even_low, jnp.where(lane < 64, even_high, odd_low), jnp.where(lane < 64, odd_low, odd_high))
    for j, piece in enumerate(pieces):
        target[pl.ds(j, count, stride=3), :] = piece


def solve_kernel(
    groups, density_ref, centers_hbm, pairs_hbm, sizes_hbm, core_ref, map_hbm, rep_hbm,
    stage_ref, arrived_ref, total_ref,
    gathered, blocks, given, field_ref, core_buf, low, high, fbuf, fock, iterate, energy_ref,
    send_sem, recv_sem, own_sem, part_send, part_recv, sum_send, sum_recv, section_send, section_recv, core_sem,
    centers_ref, pairs_ref, sizes_ref, map_ref, rep_ref, small_sem,
):
    me = lax.axis_index("grp")
    seg = lax.axis_index("segment")
    rows, flat = density_ref.shape
    orders = flow_orders(groups)
    flows = len(orders)
    stages = len(orders[0])
    half = flat // 2
    columns = half // flows
    tiles = half // LANES
    each = columns // LANES
    monomers = centers_ref.shape[1]
    width, full = map_ref.shape
    dims = pairs_ref.shape[1] // groups
    mine = dims // 2
    devices = 2 * groups
    index = seg * groups + me

    def place_of(offset):
        other = lax.rem(index + offset, devices)
        return other // groups, lax.rem(other, groups)

    barrier = pltpu.get_barrier_semaphore()
    for bit in sorted(orders[0]):
        pl.semaphore_signal(barrier, inc=1, device_id=(seg, me ^ bit), device_id_type=MESH)
    pl.semaphore_signal(barrier, inc=1, device_id=(1 - seg, me), device_id_type=MESH)
    own = []
    for f in range(flows):
        start = pl.multiple_of(seg * half + f * columns, LANES)
        source = density_ref.at[:, pl.ds(start, columns)]
        copy = pltpu.make_async_copy(source, blocks.at[f, 0], own_sem.at[f])
        copy.start()
        own.append(copy)
    fetch = pltpu.make_async_copy(core_ref.at[seg], core_buf, core_sem)
    fetch.start()
    small = []
    for i, (source, target) in enumerate((
        (centers_hbm, centers_ref), (pairs_hbm, pairs_ref), (sizes_hbm, sizes_ref), (map_hbm, map_ref), (rep_hbm, rep_ref),
    )):
        copy = pltpu.make_async_copy(source, target, small_sem.at[i])
        copy.start()
        small.append(copy)
    pl.semaphore_wait(barrier, stages + 1)

    def exchange(f, k):
        count = 1 << k
        return pltpu.make_async_remote_copy(
            src_ref=blocks.at[f, pl.ds(0, count)],
            dst_ref=blocks.at[f, pl.ds(count, count)],
            send_sem=send_sem.at[f, k],
            recv_sem=recv_sem.at[f, k],
            device_id=(seg, me ^ orders[f][k]),
            device_id_type=MESH,
        )

    for f in range(flows):
        own[f].wait()
        exchange(f, 0).start()

    for copy in small:
        copy.wait()

    place = iota((dims, 1), 0)
    positions = me * dims + jnp.where(place < mine, seg * mine + place, (1 - seg) * mine + place - mine)
    ids = pair_ids(pairs_ref, positions)
    labels = iota((dims, monomers), 1)
    is_first, is_second = [labels == i for i in ids]
    distance = jnp.zeros((dims, monomers), jnp.float32)
    for axis in range(centers_ref.shape[0]):
        row = centers_ref[axis:axis + 1, :]
        first_at = jnp.sum(jnp.where(is_first, row, 0.0), axis=1, keepdims=True)
        second_at = jnp.sum(jnp.where(is_second, row, 0.0), axis=1, keepdims=True)
        gap = 0.5 * (first_at + second_at) - row
        distance = distance + gap * gap
    weights = bf(jnp.where(is_first | is_second, 0.0, 1.0 / jnp.sqrt(distance + 1.0)))
    ordered = []
    for f in range(flows // SPLITS):
        column = iota((monomers, monomers), 1)
        slot = column // rows
        owner = jnp.full_like(column, me)
        for k, bit in enumerate(orders[f]):
            owner = owner ^ jnp.where((slot & (1 << k)) != 0, bit, 0)
        label = owner * rows + (column & (rows - 1))
        chosen = bf(jnp.where(iota((monomers, monomers), 0) == label, 1.0, 0.0))
        ordered.append(bf(dot(weights, chosen)))
    sizes = [
        jnp.sum(jnp.where(hit, sizes_ref[...].astype(jnp.float32), 0.0), axis=1, keepdims=True)[:mine]
        for hit in (is_first, is_second)
    ]

    for k in range(1, stages):
        for f in range(flows):
            exchange(f, k - 1).wait_recv()
            exchange(f, k).start()

    row_at = iota((1, full), 1)
    column_at = iota((full, 1), 0)
    eye = iota((full, full), 0) == iota((full, full), 1)
    repulsion = load_square(rep_ref, low.at[0], high.at[0], 0, 1, full)
    symmetric = 0.5 * (repulsion + repulsion.T)
    mapping = map_ref[...]
    mapping_t = mapping.T
    fetch.wait()
    for d in range(mine):
        value = load_square(core_buf, low.at[d], high.at[d], d, mine, full)
        fock[d] = 0.5 * (value + value.T)

    def partial(f, first, count):
        block = bf(blocks[f, first:first + count].astype(jnp.float32).reshape(count * rows, columns))
        return dot(ordered[f % (flows // SPLITS)][:, first * rows:(first + count) * rows], block)

    early = [partial(f, 0, groups // 2) for f in range(flows)]

    def give(f):
        return pltpu.make_async_remote_copy(
            src_ref=given.at[pl.ds(f * each, each)],
            dst_ref=field_ref.at[pl.ds(seg * tiles + f * each, each)],
            send_sem=part_send.at[f], recv_sem=part_recv.at[f],
            device_id=(1 - seg, me), device_id_type=MESH,
        )

    for f in range(flows):
        exchange(f, stages - 1).wait_recv()
        result = early[f] + partial(f, groups // 2, groups // 2)
        for t in range(each):
            piece = result[:, t * LANES:(t + 1) * LANES]
            field_ref[seg * tiles + f * each + t] = piece[:mine]
            given[f * each + t] = piece[mine:]
        give(f).start()
    for f in range(flows):
        for k in range(stages):
            exchange(f, k).wait_send()
    for f in range(flows):
        give(f).wait()

    def live(d):
        first, second = [s[d:d + 1, :] for s in sizes]
        out = []
        for at in (row_at, column_at):
            limit = jnp.where(at < width, first, second + width)
            out.append(jnp.where(at.astype(jnp.float32) < limit, 1.0, 0.0))
        return out, first + second

    def begin_all(matrices):
        masks = [live(d) for d in range(mine)]
        for d in range(mine):
            (live_row, live_column), count = masks[d]
            iterate[d] = matrices[d]() * (live_column * live_row)
        traces = [jnp.sum(jnp.where(eye, iterate[d], 0.0), axis=0, keepdims=True) for d in range(mine)]
        levels = [jnp.sum(t, axis=1, keepdims=True) / masks[d][1] for d, t in enumerate(traces)]
        sums = []
        for d in range(mine):
            shifted = iterate[d] - jnp.where(eye, levels[d] * masks[d][0][0], 0.0)
            iterate[d] = shifted
            sums.append(jnp.sum(jnp.abs(shifted), axis=0, keepdims=True))
        scales = [-1.0 / (jnp.max(t, axis=1, keepdims=True) + epsilon) for t in sums]
        for d in range(mine):
            iterate[d] = iterate[d] * scales[d]

    def step(passes):
        first, second = passes
        values = [iterate[d] for d in range(mine)]
        squares = [product(x, x, first) for x in values]
        for d in range(mine):
            x = values[d]
            iterate[d] = 1.5 * x - 0.5 * product(x, squares[d], second)

    def run(plan):
        at = 0
        while at < len(plan):
            length = 1
            while at + length < len(plan) and plan[at + length] == plan[at]:
                length += 1
            passes = plan[at]

            def body(i, carry):
                step(passes)
                return carry

            lax.fori_loop(0, length, body, 0)
            at += length

    def finish(d):
        (live_row, live_column), count = live(d)
        return 0.5 * (iterate[d] + jnp.where(eye, live_row, 0.0)), count

    def swap(part, d):
        return pltpu.make_async_remote_copy(
            src_ref=stage_ref.at[part, d], dst_ref=arrived_ref.at[d],
            send_sem=section_send.at[d], recv_sem=section_recv.at[d],
            device_id=(1 - seg, me), device_id_type=MESH,
        )

    fields = [load_field(field_ref, fbuf.at[d], d, width) for d in range(mine)]
    fields = [0.5 * (field + field.T) for field in fields]
    lefts = [product(field, mapping, 3) for field in fields]
    for d in range(mine):
        fock[d] = fock[d] + product(mapping_t, lefts[d], 3)
    begin_all([lambda d=d: fock[d] for d in range(mine)])
    for d in range(mine):
        store_square(stage_ref.at[0, d], fock[d], low.at[d], high.at[d], full)

    @pl.when(seg == 1)
    def _():
        for d in range(mine):
            swap(0, d).start()

    run(FIRST_PLAN)
    def rebuilt(d):
        density, count = finish(d)
        occupied = jnp.sum(jnp.where(eye, density, 0.0), axis=1, keepdims=True)
        coulomb = jnp.sum(symmetric * occupied, axis=0, keepdims=True)
        change = jnp.where(eye, coulomb, 0.0) - 0.5 * symmetric * density
        core_fock = fock[d]
        fock[d] = 2.0 * core_fock + change
        return core_fock + change

    begin_all([functools.partial(rebuilt, d) for d in range(mine)])
    run(LAST_PLAN)
    partials = jnp.zeros((1, full), jnp.float32)
    for d in range(mine):
        density, count = finish(d)
        iterate[d] = density
        partials = partials + jnp.sum(density * fock[d], axis=0, keepdims=True) * (0.5 / count)
    energy = jnp.sum(partials, axis=1, keepdims=True)
    energy_ref[...] = jnp.broadcast_to(energy, energy_ref.shape)
    gathered[index] = energy_ref[...]
    copies = []
    for offset in range(1, devices):
        copy = pltpu.make_async_remote_copy(
            src_ref=energy_ref, dst_ref=gathered.at[index], send_sem=sum_send.at[offset], recv_sem=sum_recv.at[offset],
            device_id=place_of(offset), device_id_type=MESH,
        )
        copy.start()
        copies.append(copy)
    for d in range(mine):
        store_square(stage_ref.at[1, d], iterate[d], low.at[d], high.at[d], full)

        @pl.when(seg == 0)
        def _():
            swap(1, d).start()

    for copy in copies:
        copy.wait()
    total_ref[...] = jnp.sum(gathered[...], axis=0)
    for d in range(mine):
        swap(1 - seg, d).wait()


def solve(groups, density, centers, pairs, sizes, core, mapping, repulsion):
    rows, total = density.shape
    flows = len(flow_orders(groups))
    stages = groups.bit_length() - 1
    half = total // 2
    devices = 2 * groups
    width, full = mapping.shape
    mine = pairs.shape[1] // groups // 2
    tiles = full * full // LANES
    vmem = pl.BlockSpec(memory_space=pltpu.VMEM)
    anywhere = pl.BlockSpec(memory_space=pl.ANY)
    return pl.pallas_call(
        functools.partial(solve_kernel, groups),
        out_shape=(
            KEEP((2, mine, tiles, LANES), jnp.float32),
            KEEP((mine, tiles, LANES), jnp.float32),
            KEEP((1, LANES), jnp.float32),
        ),
        in_specs=[anywhere] * 7,
        out_specs=(vmem, vmem, vmem),
        scratch_shapes=[
            pltpu.VMEM((devices, 1, LANES), jnp.float32),
            pltpu.VMEM((flows, groups, rows, half // flows), jnp.bfloat16),
            pltpu.VMEM((half // LANES, mine, LANES), jnp.float32),
            pltpu.VMEM((total // LANES, mine, LANES), jnp.float32),
            pltpu.VMEM((tiles * mine, LANES), jnp.float32),
            pltpu.VMEM((mine, full, LANES), jnp.float32),
            pltpu.VMEM((mine, full, LANES), jnp.float32),
            pltpu.VMEM((mine, width, LANES), jnp.float32),
            pltpu.VMEM((mine, full, full), jnp.float32),
            pltpu.VMEM((mine, full, full), jnp.float32),
            pltpu.VMEM((1, LANES), jnp.float32),
            pltpu.SemaphoreType.DMA((flows, stages)),
            pltpu.SemaphoreType.DMA((flows, stages)),
            pltpu.SemaphoreType.DMA((flows,)),
            pltpu.SemaphoreType.DMA((flows,)),
            pltpu.SemaphoreType.DMA((flows,)),
            pltpu.SemaphoreType.DMA((devices,)),
            pltpu.SemaphoreType.DMA((devices,)),
            pltpu.SemaphoreType.DMA((mine,)),
            pltpu.SemaphoreType.DMA((mine,)),
            pltpu.SemaphoreType.DMA,
            *[pltpu.VMEM(small.shape, small.dtype) for small in (centers, pairs, sizes, mapping, repulsion)],
            pltpu.SemaphoreType.DMA((5,)),
        ],
        compiler_params=pltpu.CompilerParams(collective_id=0, has_side_effects=True),
    )(density, centers, pairs, sizes, core, mapping, repulsion)


def merge_kernel(share, stage_ref, arrived_ref, sum_ref, out_ref, total_ref):
    seg = lax.axis_index("segment")
    half = pl.program_id(0)
    mine, tiles, _ = arrived_ref.shape

    @pl.when(half == 0)
    def _():
        total_ref[...] = sum_ref[:, :1] * share

    @pl.when(half == seg)
    def _():
        for d in range(mine):
            out_ref[0, pl.ds(d, tiles, stride=mine), :] = stage_ref[seg, d]

    @pl.when(half != seg)
    def _():
        for d in range(mine):
            out_ref[0, pl.ds(d, tiles, stride=mine), :] = arrived_ref[d]


def merge(share, stage, arrived, gathered):
    mine, tiles, _ = arrived.shape
    vmem = pl.BlockSpec(memory_space=pltpu.VMEM)
    return pl.pallas_call(
        functools.partial(merge_kernel, share),
        out_shape=(
            jax.ShapeDtypeStruct((2, tiles * mine, LANES), jnp.float32),
            jax.ShapeDtypeStruct((1, 1), jnp.float32),
        ),
        grid=(2,),
        in_specs=[vmem, vmem, vmem],
        out_specs=(
            pl.BlockSpec((1, tiles * mine, LANES), lambda i: (i, 0, 0)),
            pl.BlockSpec((1, 1), lambda i: (0, 0)),
        ),
        compiler_params=pltpu.CompilerParams(vmem_limit_bytes=16 << 20),
    )(stage, arrived, gathered)


def on_device(groups, monomer_density, monomer_centers, dimer_pairs, basis_sizes, dimer_core, esp_map, repulsion):
    dims, flat = dimer_core.shape
    mine = dims // 2
    tiles = flat // LANES
    core = dimer_core.reshape(2, mine, tiles, LANES).transpose(0, 2, 1, 3).reshape(2, tiles * mine, LANES)
    stage, arrived, gathered = solve(
        groups, monomer_density, monomer_centers, dimer_pairs, basis_sizes.reshape(1, -1), core, esp_map,
        repulsion.reshape(tiles, LANES),
    )
    section, total = merge(1.0 / dimer_pairs.shape[1], stage, arrived, gathered)
    section = section.reshape(2, tiles, mine, LANES).transpose(0, 2, 1, 3).reshape(1, dims, flat)
    return section, total[0, 0]


def solution(mesh):
    in_specs = (P("grp", None), P(), P(), P(), P("grp", None), P(), P())
    out_specs = (P("segment", "grp", None), P())
    return jax.shard_map(
        functools.partial(on_device, mesh.shape["grp"]), mesh=mesh, in_specs=in_specs, out_specs=out_specs, check_vma=False
    )
```
